32 devices in a mesh: groups: 2 (over y), frames: 16 (over z, x, core).
Axes of the slice: x: 2, y: 2, z: 4, core: 2. Of those that a mesh axis runs over, the one named last changes fastest.
Arguments:
- video_frames: bfloat16 [64, 1024, 1024], P(('groups', 'frames')), parts along dimension 0, may hold values from -6 to 6
- segments: int32 [64], P('groups'), parts along dimension 0, may hold values from 0 to 3, never falling along the last dimension, each value on 1 to 29 neighbouring positions
- ref_pick: int32 [8], P('groups'), parts along dimension 0, may hold values from 0 to 4095
- band_taps: bfloat16 [32], replicated, may hold values from -2 to 2
Outputs:
- motion: float32 [64, 256, 256], P(('groups', 'frames')), parts along dimension 0
The draws below stay inside these ranges and needn't reach their ends.
There are 2 independent parts, one for each index of `groups`. The reference program is written for one: setup_inputs(seed, part) draws one part's arguments, and reference() takes and returns one part's arrays. A program takes and returns all parts, laid end to end along the dimension named above; an argument that names none is the same for every part. Nothing has to cross between parts.
Inputs may be any that keep to these rules, and one draw needn't show every extreme that they name: Segment numbers never fall along the frames; each of the 4 segments holds 1 to 29 frames and one holds exactly 29.
All inputs are finite; a program needn't handle non-finite values.
Results may differ from the reference program's by a relative error of at most 0.012.
Values may be sent and summed in bfloat16 or wider, within the bound.
A program may use at most 128 MiB of HBM per device.

```python
import math
import jax
import jax.numpy as jnp
import numpy as np
from jax import lax

IMG = 1024
ORIENT = 4
TAPS = 32
NSEG = 4
QUART = 256
FRAMES = 32
SEG_MOST = 29


def plant(values, key, least, high):
    longest = values.shape.index(max(values.shape))
    spots = []
    for shift in (0, 1):
        where = [jax.random.randint(jax.random.fold_in(key, axis), (), 0, length) for axis, length in enumerate(values.shape)]
        where[longest] = (where[longest] + shift) % values.shape[longest]
        spots.append(tuple(where))
    return values.at[spots[0]].set(least).at[spots[1]].set(high)


def block_scale(stream_key, dims, shards, low, high):
    def one(dim, parts):
        draws = jax.random.uniform(jax.random.fold_in(jax.random.fold_in(stream_key, 6), dim), (parts,), jnp.float32, low / len(shards), high / len(shards))
        return jnp.repeat(jnp.exp(draws), dims[dim] // parts).reshape((-1,) + (1,) * (len(dims) - dim - 1))

    factor_of = one(*shards[0])
    for cut in shards[1:]:
        factor_of = factor_of * one(*cut)
    return factor_of


def length_profile(number_of, total, limit, lean):
    portions = [(1 << 20) // math.isqrt(rank ** lean) + 1 for rank in range(2, number_of + 1)]
    rest, holding = total - limit - (number_of - 1), [1] * (number_of - 1)
    while rest > 0:
        free = [i for i in range(number_of - 1) if holding[i] < limit]
        mass, remaining = sum([portions[i] for i in free]), rest
        for i in free:
            more = min(limit - holding[i], max(1, remaining * portions[i] // mass), rest)
            holding[i] = holding[i] + more
            rest = rest - more
    return np.array([limit] + holding)


def ragged(rng, amount, total, reach, slope):
    if amount == 2:
        one = jax.random.randint(rng, (), max(1, total - reach), min(reach, total - 1) + 1)
        return jnp.stack([one, total - one])
    tallies = jnp.asarray(length_profile(amount, total, reach, slope), jnp.int32)
    couples = (amount - 1) // 2
    source_of, receiver = tallies[1:1 + 2 * couples:2], tallies[2:2 + 2 * couples:2]
    slack = jnp.minimum(source_of - 1, reach - receiver)
    moved = jax.random.randint(jax.random.fold_in(rng, 1), (couples,), 0, 1 << 20) % (slack + 1)
    tallies = tallies.at[1:1 + 2 * couples:2].set(source_of - moved).at[2:2 + 2 * couples:2].set(receiver + moved)
    return tallies[jax.random.permutation(jax.random.fold_in(rng, 2), amount)]


def scatter_about(stream_key, extent, width, bound, cuts=(), held_as=jnp.bfloat16):
    result = width * jax.random.normal(stream_key, extent, jnp.float32)
    if cuts:
        result = result * block_scale(stream_key, extent, cuts, -0.22, 0.18)
    return jnp.clip(result, -bound, bound).astype(held_as)


def setup_inputs(seed: int = 0, part: int = 0) -> dict:
    seeds = jax.random.split(jax.random.key(seed), 5)
    part_keys = jax.random.split(jax.random.fold_in(seeds[4], part), 5)
    return {
        "video_frames": scatter_about(part_keys[0], (FRAMES, IMG, IMG), 1.0, 6.0, ((0, 16),)),
        "segments": jnp.searchsorted(jnp.cumsum(ragged(part_keys[1], NSEG, FRAMES, SEG_MOST, 1)), jnp.arange(FRAMES), side="right").astype(jnp.int32),
        "ref_pick": plant(jax.random.randint(part_keys[2], (NSEG,), 0, 4096), jax.random.fold_in(part_keys[2], 1), 0, 4095).astype(jnp.int32),
        "band_taps": scatter_about(seeds[3], (TAPS,), 0.35, 2.0),
    }


blur_sigma = 2.0
gabor_sigma = 2.0
wave_number = math.pi / 2.0
gabor_gain = 2.0

def make_down(full_size, quarter):
    position = jnp.arange(quarter, dtype=jnp.float32)[:, None]
    columns = jnp.arange(full_size, dtype=jnp.float32)[None, :]
    offset_grid = columns - 4.0 * position - 1.5
    weight = jnp.exp(-offset_grid * offset_grid / (2.0 * blur_sigma * blur_sigma))
    return (weight / lax.optimization_barrier(jnp.sum(weight, axis=1, keepdims=True))).astype(jnp.bfloat16)

def gabor_tables(quarter, orient):
    position = jnp.arange(quarter, dtype=jnp.float32)
    offset_grid = position[None, :] - position[:, None]
    envelope = gabor_gain * jnp.exp(-offset_grid * offset_grid / (2.0 * gabor_sigma * gabor_sigma))
    angles = jnp.arange(orient, dtype=jnp.float32) * (math.pi / orient)
    wave_x = wave_number * jnp.cos(angles)
    wave_y = wave_number * jnp.sin(angles)
    phase_y = wave_y[:, None, None] * offset_grid[None]
    left_table = jnp.stack([envelope * jnp.cos(phase_y), envelope * jnp.sin(phase_y)], axis=2)
    left_table = left_table.reshape(orient * quarter * 2, quarter).astype(jnp.bfloat16)
    phase_x = wave_x[:, None, None] * (-offset_grid)[None]
    real_part = envelope * jnp.cos(phase_x)
    imag_part = envelope * jnp.sin(phase_x)
    upper_half = jnp.concatenate([real_part, imag_part], axis=2)
    lower_half = jnp.concatenate([-imag_part, real_part], axis=2)
    right_table = jnp.concatenate([upper_half, lower_half], axis=1).astype(jnp.bfloat16)
    return (left_table, right_table)

def frame_coeff(single, down_matrix, left_table, right_table):
    half_done = jnp.dot(single, down_matrix.T, preferred_element_type=jnp.float32).astype(jnp.bfloat16)
    reduced = jnp.dot(down_matrix, half_done, preferred_element_type=jnp.float32).astype(jnp.bfloat16)
    stacked = jnp.dot(left_table, reduced, preferred_element_type=jnp.float32).astype(jnp.bfloat16)
    quarter = reduced.shape[0]
    orient = right_table.shape[0]
    stacked = stacked.reshape(orient, quarter, 2 * quarter)
    return jnp.einsum('oya,oab->oyb', stacked.astype(jnp.float32), right_table.astype(jnp.float32)).astype(jnp.bfloat16)

def phase_terms(coeffs, per_frame):
    quarter = coeffs.shape[-1] // 2
    coeff_real = coeffs[..., :quarter].astype(jnp.float32)
    coeff_imag = coeffs[..., quarter:].astype(jnp.float32)
    ref_real = per_frame[..., :quarter].astype(jnp.float32)
    ref_imag = per_frame[..., quarter:].astype(jnp.float32)
    prod_real = coeff_real * ref_real + coeff_imag * ref_imag
    prod_imag = coeff_imag * ref_real - coeff_real * ref_imag
    phase_signal = (prod_imag / jnp.sqrt(prod_real * prod_real + prod_imag * prod_imag + 1.0)).astype(jnp.bfloat16)
    amplitude = coeff_real * coeff_real + coeff_imag * coeff_imag
    return (phase_signal, amplitude)

def taps_matrix(band_taps, frame_count):
    frame_index = jnp.arange(frame_count, dtype=jnp.int32)
    lag_grid = frame_index[:, None] - frame_index[None, :]
    one_hot = (lag_grid[:, :, None] == jnp.arange(band_taps.shape[0], dtype=jnp.int32)[None, None, :]).astype(jnp.float32)
    return jnp.einsum('tsk,k->ts', one_hot, band_taps.astype(jnp.float32)).astype(jnp.bfloat16)

def segment_refs(segments, ref_pick, segment_count):
    numbers = jnp.arange(segment_count, dtype=jnp.int32)
    starts = lax.optimization_barrier(jnp.sum((segments[None, :] < numbers[:, None]).astype(jnp.int32), axis=1))
    counts = lax.optimization_barrier(jnp.sum((segments[None, :] == numbers[:, None]).astype(jnp.int32), axis=1))
    return (starts + ref_pick % counts).astype(jnp.int32)

def reference(video_frames, segments, ref_pick, band_taps):
    down_matrix = make_down(IMG, QUART)
    left_table, right_table = gabor_tables(QUART, ORIENT)
    coeffs = lax.map(lambda single: frame_coeff(single, down_matrix, left_table, right_table), video_frames)
    ref_frames = segment_refs(segments, ref_pick, NSEG)
    ref_coeffs = coeffs[ref_frames]
    per_frame = ref_coeffs[segments]
    phase_signal, amplitude = phase_terms(coeffs, per_frame)
    matrix = taps_matrix(band_taps, FRAMES)
    filtered = jnp.dot(matrix, phase_signal.reshape(FRAMES, -1), preferred_element_type=jnp.float32)
    filtered = filtered.astype(jnp.bfloat16).reshape(phase_signal.shape).astype(jnp.float32)
    return lax.optimization_barrier(jnp.sum(amplitude * filtered, axis=1)) / (lax.optimization_barrier(jnp.sum(amplitude, axis=1)) + 1.0)
```

```python
import math

import jax
import numpy as np
import jax.numpy as jnp
from jax import lax
from jax.experimental import pallas as pl
from jax.experimental.pallas import tpu as pltpu
from jax.sharding import PartitionSpec as P

IMG = 1024
ORIENT = 4
NSEG = 4
QUART = 256


blur_sigma = 2.0
gabor_sigma = 2.0
wave_number = math.pi / 2.0
gabor_gain = 2.0


def spread(x, axis, root):
    mine = lax.axis_index(axis) == root
    return lax.psum(jnp.where(mine, x, jnp.zeros_like(x)), axis)


def make_down(full_size, quarter):
    position = jnp.arange(quarter, dtype=jnp.float32)[:, None]
    columns = jnp.arange(full_size, dtype=jnp.float32)[None, :]
    offset_grid = columns - 4.0 * position - 1.5
    weight = jnp.exp(-offset_grid * offset_grid / (2.0 * blur_sigma * blur_sigma))
    return (weight / jnp.sum(weight, axis=1, keepdims=True)).astype(jnp.bfloat16)


def gabor_tables(quarter, orient):
    position = jnp.arange(quarter, dtype=jnp.float32)
    offset_grid = position[None, :] - position[:, None]
    envelope = gabor_gain * jnp.exp(-offset_grid * offset_grid / (2.0 * gabor_sigma * gabor_sigma))
    angles = jnp.arange(orient, dtype=jnp.float32) * (math.pi / orient)
    wave_x = wave_number * jnp.cos(angles)
    wave_y = wave_number * jnp.sin(angles)
    phase_y = wave_y[:, None, None] * offset_grid[None]
    left_table = jnp.stack([envelope * jnp.cos(phase_y), envelope * jnp.sin(phase_y)], axis=2)
    left_table = left_table.reshape(orient * quarter * 2, quarter).astype(jnp.bfloat16)
    phase_x = wave_x[:, None, None] * (-offset_grid)[None]
    real_part = envelope * jnp.cos(phase_x)
    imag_part = envelope * jnp.sin(phase_x)
    upper_half = jnp.concatenate([real_part, imag_part], axis=2)
    lower_half = jnp.concatenate([-imag_part, real_part], axis=2)
    right_table = jnp.concatenate([upper_half, lower_half], axis=1).astype(jnp.bfloat16)
    return (left_table, right_table)


def phase_terms(coeffs, per_frame):
    quarter = coeffs.shape[-1] // 2
    coeff_real = coeffs[..., :quarter].astype(jnp.float32)
    coeff_imag = coeffs[..., quarter:].astype(jnp.float32)
    ref_real = per_frame[..., :quarter].astype(jnp.float32)
    ref_imag = per_frame[..., quarter:].astype(jnp.float32)
    prod_real = coeff_real * ref_real + coeff_imag * ref_imag
    prod_imag = coeff_imag * ref_real - coeff_real * ref_imag
    phase_signal = (
        prod_imag / jnp.sqrt(prod_real * prod_real + prod_imag * prod_imag + 1.0)
    ).astype(jnp.bfloat16)
    amplitude = coeff_real * coeff_real + coeff_imag * coeff_imag
    return (phase_signal, amplitude)


def taps_matrix(band_taps, frame_count):
    frame_index = jnp.arange(frame_count, dtype=jnp.int32)
    lag_grid = frame_index[:, None] - frame_index[None, :]
    one_hot = (
        lag_grid[:, :, None] == jnp.arange(band_taps.shape[0], dtype=jnp.int32)[None, None, :]
    ).astype(jnp.float32)
    return jnp.einsum("tsk,k->ts", one_hot, band_taps.astype(jnp.float32)).astype(jnp.bfloat16)


def segment_refs(segments, ref_pick, segment_count):
    numbers = jnp.arange(segment_count, dtype=jnp.int32)
    starts = jnp.sum((segments[None, :] < numbers[:, None]).astype(jnp.int32), axis=1)
    counts = jnp.sum((segments[None, :] == numbers[:, None]).astype(jnp.int32), axis=1)
    return starts + ref_pick % counts


def body(video_frames, segments, ref_pick, band_taps):
    frames_here = video_frames.shape[0]
    down_matrix = make_down(IMG, QUART)
    left_table, right_table = gabor_tables(QUART, ORIENT)

    def reduce_frames(pictures):
        half_done = jnp.einsum(
            "nia,qa->niq", pictures, down_matrix, preferred_element_type=jnp.float32
        ).astype(jnp.bfloat16)
        return jnp.einsum(
            "qi,nik->nqk", down_matrix, half_done, preferred_element_type=jnp.float32
        ).astype(jnp.bfloat16)

    def filter_frames(reduced):
        stacked = jnp.einsum(
            "ra,nak->nrk", left_table, reduced, preferred_element_type=jnp.float32
        ).astype(jnp.bfloat16)
        stacked = stacked.reshape(reduced.shape[0], ORIENT, QUART, 2 * QUART)
        return jnp.einsum(
            "noya,oab->noyb", stacked, right_table, preferred_element_type=jnp.float32
        ).astype(jnp.bfloat16)

    small_own = reduce_frames(video_frames)
    coeff_own = filter_frames(small_own)
    ref_frames = segment_refs(segments, ref_pick, NSEG)
    gathered = []
    for segment in range(NSEG):
        root_index = ref_frames[segment] // frames_here
        local_index = ref_frames[segment] % frames_here
        payload = lax.dynamic_index_in_dim(video_frames, local_index, 0, keepdims=False)
        gathered.append(spread(payload, "frames", root_index))
    ref_coeff = filter_frames(reduce_frames(jnp.stack(gathered)))
    first_frame = lax.axis_index("frames") * frames_here
    own_ids = lax.dynamic_slice_in_dim(segments, first_frame, frames_here)
    select = (own_ids[:, None] == jnp.arange(NSEG, dtype=jnp.int32)[None, :]).astype(jnp.bfloat16)
    per_frame = jnp.dot(select, ref_coeff.reshape(NSEG, -1), preferred_element_type=jnp.float32)
    per_frame = per_frame.astype(jnp.bfloat16).reshape(coeff_own.shape)
    phase_signal, amplitude = phase_terms(coeff_own, per_frame)
    phase_signal = phase_signal.reshape(frames_here, ORIENT, QUART * QUART)
    pixel_rows = lax.all_to_all(phase_signal, "frames", split_axis=2, concat_axis=0, tiled=True)
    matrix = taps_matrix(band_taps, pixel_rows.shape[0])
    filtered = jnp.einsum(
        "ts,sop->top", matrix, pixel_rows, preferred_element_type=jnp.float32
    ).astype(jnp.bfloat16)
    filtered = lax.all_to_all(filtered, "frames", split_axis=0, concat_axis=2, tiled=True)
    filtered = filtered.reshape(frames_here, ORIENT, QUART, QUART).astype(jnp.float32)
    return jnp.sum(amplitude * filtered, axis=1) / (jnp.sum(amplitude, axis=1) + 1.0)


REACH = 32


def down_table():
    position = np.arange(QUART, dtype=np.float32)[:, None]
    columns = np.arange(IMG, dtype=np.float32)[None, :]
    offset = columns - np.float32(4.0) * position - np.float32(1.5)
    weight = np.exp(-offset * offset / np.float32(2.0 * blur_sigma * blur_sigma))
    return (weight / np.sum(weight, axis=1, keepdims=True)).astype(jnp.bfloat16)


def waves():
    angles = np.arange(ORIENT, dtype=np.float32) * np.float32(math.pi / ORIENT)
    return np.float32(wave_number) * np.cos(angles), np.float32(wave_number) * np.sin(angles)


def gabor_envelope(offset):
    return np.float32(gabor_gain) * np.exp(-offset * offset / np.float32(2.0 * gabor_sigma * gabor_sigma))


def left_window(rows):
    offset = (
        np.arange(rows + 2 * REACH, dtype=np.float32)[None, :]
        - REACH
        - np.arange(rows, dtype=np.float32)[:, None]
    )
    envelope = gabor_envelope(offset)
    phase = waves()[1][:, None, None] * offset[None]
    table = np.stack([envelope * np.cos(phase), envelope * np.sin(phase)], axis=1)
    return table.reshape(ORIENT * 2 * rows, -1).astype(jnp.bfloat16)


def right_tables():
    position = np.arange(QUART, dtype=np.float32)
    offset = position[:, None] - position[None, :]
    envelope = gabor_envelope(offset)
    phase = waves()[0][:, None, None] * offset[None]
    real, imag = envelope * np.cos(phase), envelope * np.sin(phase)
    upper = np.concatenate([real, imag], axis=2)
    lower = np.concatenate([-imag, real], axis=2)
    return np.stack([upper, lower], axis=1).astype(jnp.bfloat16)


def make_kernel(parts, here, rows):
    frames = parts * here
    window = rows + 2 * REACH
    total = frames * rows

    def kernel(
        refs, taps, video_hbm, down_hbm, down_t_hbm, left, right_hbm, out,
        video, down, down_t, right, half, reduced, gathered, stacked, coeffs,
        phase, matrix, numer, denom, moved, landed,
        load_sem, send_a, recv_a, send_b, recv_b,
    ):
        me = lax.axis_index("frames")
        barrier = pltpu.get_barrier_semaphore()

        def peer(j):
            return lax.rem(me + j, parts)

        def source(j):
            return lax.rem(me + parts - j, parts)

        loads = [
            pltpu.make_async_copy(down_t_hbm, down_t, load_sem.at[0]),
        ]
        for n in range(here):
            loads.append(pltpu.make_async_copy(video_hbm.at[n], video.at[n], load_sem.at[1 + n]))
        loads.append(pltpu.make_async_copy(down_hbm, down, load_sem.at[1 + here]))
        loads.append(pltpu.make_async_copy(right_hbm, right, load_sem.at[2 + here]))
        for copy in loads:
            copy.start()

        @pl.loop(1, parts)
        def _(j):
            pl.semaphore_signal(barrier, inc=1, device_id={"frames": peer(j)})

        edge = jnp.zeros((here, REACH, QUART), jnp.bfloat16)
        reduced[:, :REACH, :] = edge
        reduced[:, REACH + QUART :, :] = edge

        loads[0].wait()
        for n in range(here):
            loads[1 + n].wait()
            half[n] = jnp.dot(
                video[n], down_t[...], preferred_element_type=jnp.float32
            ).astype(jnp.bfloat16)
        loads[1 + here].wait()
        for n in range(here):
            reduced[n, REACH : REACH + QUART, :] = jnp.dot(
                down[...], half[n], preferred_element_type=jnp.float32
            ).astype(jnp.bfloat16)

        pl.semaphore_wait(barrier, parts - 1)

        def spread_copy(j):
            to = peer(j)
            return pltpu.make_async_remote_copy(
                src_ref=reduced.at[:, pl.ds(pl.multiple_of(to * rows, rows), window), :],
                dst_ref=gathered.at[pl.ds(me * here, here)],
                send_sem=send_a.at[j],
                recv_sem=recv_a.at[j],
                device_id={"frames": to},
            )

        @pl.loop(1, parts)
        def _(j):
            spread_copy(j).start()

        lag = lax.broadcasted_iota(jnp.int32, (frames, frames), 0) - lax.broadcasted_iota(
            jnp.int32, (frames, frames), 1
        )
        toeplitz = jnp.zeros((frames, frames), jnp.float32)
        tap_row = taps[...].astype(jnp.float32)
        for k in range(min(taps.shape[1], frames)):
            toeplitz = jnp.where(lag == k, tap_row[:, k : k + 1], toeplitz)
        owner = lax.broadcasted_iota(jnp.int32, (total, frames), 0) // rows
        repeat = jnp.where(
            owner == lax.broadcasted_iota(jnp.int32, (total, frames), 1), 1.0, 0.0
        ).astype(jnp.bfloat16)
        tall = jnp.dot(
            repeat, toeplitz.astype(jnp.bfloat16), preferred_element_type=jnp.float32
        ).astype(jnp.bfloat16)
        wide = lax.dot_general(
            tall, repeat, (((1,), (1,)), ((), ())), preferred_element_type=jnp.float32
        )
        same = (
            lax.broadcasted_iota(jnp.int32, (total, total), 0) % rows
            == lax.broadcasted_iota(jnp.int32, (total, total), 1) % rows
        )
        matrix[...] = jnp.where(same, wide, 0.0).astype(jnp.bfloat16)

        def stack_one(t, block):
            stacked[t] = (
                jnp.dot(left[...], block, preferred_element_type=jnp.float32)
                .astype(jnp.bfloat16)
                .reshape(ORIENT * 2, rows, QUART)
            )

        own = pl.ds(pl.multiple_of(me * rows, rows), window)
        for n in range(here):
            stack_one(me * here + n, reduced[n, own, :])

        @pl.loop(1, parts)
        def _(j):
            spread_copy(j).wait_recv()
            base = source(j) * here
            for n in range(here):
                stack_one(base + n, gathered[base + n])

        loads[2 + here].wait()
        step = frames // 4
        for o in range(ORIENT):
            for part in range(4):
                where = slice(part * step, (part + 1) * step)
                value = jnp.dot(
                    stacked[where, 2 * o].reshape(step * rows, QUART),
                    right[o, 0],
                    preferred_element_type=jnp.float32,
                ) + jnp.dot(
                    stacked[where, 2 * o + 1].reshape(step * rows, QUART),
                    right[o, 1],
                    preferred_element_type=jnp.float32,
                )
                coeffs[where, o] = value.astype(jnp.bfloat16).reshape(step, rows, 2 * QUART)

        @pl.loop(0, frames)
        def _(t):
            ref = refs[t]
            ones = coeffs[t].astype(jnp.float32)
            base = coeffs[ref].astype(jnp.float32)
            real, imag = ones[..., :QUART], ones[..., QUART:]
            ref_real, ref_imag = base[..., :QUART], base[..., QUART:]
            prod_real = real * ref_real + imag * ref_imag
            prod_imag = imag * ref_real - real * ref_imag
            signal = prod_imag * lax.rsqrt(prod_real * prod_real + prod_imag * prod_imag + 1.0)
            phase[:, t] = signal.astype(jnp.bfloat16)
            denom[t] = jnp.sum(real * real + imag * imag, axis=0) + 1.0

        for o in range(ORIENT):
            filtered = (
                jnp.dot(
                    matrix[...],
                    phase[o].reshape(total, QUART),
                    preferred_element_type=jnp.float32,
                )
                .astype(jnp.bfloat16)
                .astype(jnp.float32)
                .reshape(frames, rows, QUART)
            )
            real = coeffs[:, o, :, :QUART].astype(jnp.float32)
            imag = coeffs[:, o, :, QUART:].astype(jnp.float32)
            term = (real * real + imag * imag) * filtered
            if o == 0:
                numer[...] = term
            elif o < ORIENT - 1:
                numer[...] += term
            else:
                moved[...] = ((numer[...] + term) / denom[...]).astype(jnp.bfloat16)

        here_rows = pl.ds(pl.multiple_of(me * rows, rows), rows)

        def return_copy(j):
            to = peer(j)
            return pltpu.make_async_remote_copy(
                src_ref=moved.at[pl.ds(to * here, here)],
                dst_ref=landed.at[:, here_rows, :],
                send_sem=send_b.at[j],
                recv_sem=recv_b.at[j],
                device_id={"frames": to},
            )

        @pl.loop(1, parts)
        def _(j):
            return_copy(j).start()

        landed[:, here_rows, :] = moved[pl.ds(me * here, here)]

        @pl.loop(1, parts)
        def _(j):
            spread_copy(j).wait_send()

        @pl.loop(1, parts)
        def _(j):
            return_copy(j).wait_recv()

        out[...] = landed[...].astype(jnp.float32)

        @pl.loop(1, parts)
        def _(j):
            return_copy(j).wait_send()

    bf16, f32, dma = jnp.bfloat16, jnp.float32, pltpu.SemaphoreType.DMA
    anywhere = pl.BlockSpec(memory_space=pl.ANY)
    vmem = pl.BlockSpec(memory_space=pltpu.VMEM)
    return pl.pallas_call(
        kernel,
        out_shape=jax.ShapeDtypeStruct((here, QUART, QUART), f32),
        in_specs=[pl.BlockSpec(memory_space=pltpu.SMEM), vmem, anywhere, anywhere, anywhere, vmem, anywhere],
        out_specs=vmem,
        scratch_shapes=[
            pltpu.VMEM((here, IMG, IMG), bf16),
            pltpu.VMEM((QUART, IMG), bf16),
            pltpu.VMEM((IMG, QUART), bf16),
            pltpu.VMEM((ORIENT, 2, QUART, 2 * QUART), bf16),
            pltpu.VMEM((here, IMG, QUART), bf16),
            pltpu.VMEM((here, QUART + 2 * REACH, QUART), bf16),
            pltpu.VMEM((frames, window, QUART), bf16),
            pltpu.VMEM((frames, ORIENT * 2, rows, QUART), bf16),
            pltpu.VMEM((frames, ORIENT, rows, 2 * QUART), bf16),
            pltpu.VMEM((ORIENT, frames, rows, QUART), bf16),
            pltpu.VMEM((total, total), bf16),
            pltpu.VMEM((frames, rows, QUART), f32),
            pltpu.VMEM((frames, rows, QUART), f32),
            pltpu.VMEM((frames, rows, QUART), bf16),
            pltpu.VMEM((here, QUART, QUART), bf16),
            dma((3 + here,)),
            dma((parts,)),
            dma((parts,)),
            dma((parts,)),
            dma((parts,)),
        ],
        compiler_params=pltpu.CompilerParams(
            collective_id=0, has_side_effects=True, vmem_limit_bytes=60 * 1024 * 1024
        ),
    )


def kernel_body(parts, video_frames, segments, ref_pick, band_taps):
    here = video_frames.shape[0]
    rows = QUART // parts
    ref_frames = segment_refs(segments, ref_pick, NSEG)
    numbers = jnp.arange(NSEG, dtype=jnp.int32)
    per_frame = jnp.sum(jnp.where(segments[:, None] == numbers[None, :], ref_frames[None, :], 0), axis=1)
    down = down_table()
    return make_kernel(parts, here, rows)(
        per_frame.astype(jnp.int32),
        band_taps[None, :],
        video_frames,
        jnp.asarray(down),
        jnp.asarray(np.ascontiguousarray(down.T)),
        jnp.asarray(left_window(rows)),
        jnp.asarray(right_tables()),
    )


def solution(mesh):
    parts = mesh.shape["frames"]
    if QUART % parts == 0 and (QUART // parts) % 16 == 0:
        chosen = lambda *args: kernel_body(parts, *args)
    else:
        chosen = body
    in_specs = (P(("groups", "frames"), None, None), P("groups"), P("groups"), P())
    out_specs = P(("groups", "frames"), None, None)
    return jax.shard_map(chosen, mesh=mesh, in_specs=in_specs, out_specs=out_specs, check_vma=False)
```

```python
import math

import jax
import numpy as np
import jax.numpy as jnp
from jax import lax
from jax.experimental import pallas as pl
from jax.experimental.pallas import tpu as pltpu
from jax.sharding import PartitionSpec as P

IMG = 1024
ORIENT = 4
NSEG = 4
QUART = 256


blur_sigma = 2.0
gabor_sigma = 2.0
wave_number = math.pi / 2.0
gabor_gain = 2.0


def spread(x, axis, root):
    mine = lax.axis_index(axis) == root
    return lax.psum(jnp.where(mine, x, jnp.zeros_like(x)), axis)


def make_down(full_size, quarter):
    position = jnp.arange(quarter, dtype=jnp.float32)[:, None]
    columns = jnp.arange(full_size, dtype=jnp.float32)[None, :]
    offset_grid = columns - 4.0 * position - 1.5
    weight = jnp.exp(-offset_grid * offset_grid / (2.0 * blur_sigma * blur_sigma))
    return (weight / jnp.sum(weight, axis=1, keepdims=True)).astype(jnp.bfloat16)


def gabor_tables(quarter, orient):
    position = jnp.arange(quarter, dtype=jnp.float32)
    offset_grid = position[None, :] - position[:, None]
    envelope = gabor_gain * jnp.exp(-offset_grid * offset_grid / (2.0 * gabor_sigma * gabor_sigma))
    angles = jnp.arange(orient, dtype=jnp.float32) * (math.pi / orient)
    wave_x = wave_number * jnp.cos(angles)
    wave_y = wave_number * jnp.sin(angles)
    phase_y = wave_y[:, None, None] * offset_grid[None]
    left_table = jnp.stack([envelope * jnp.cos(phase_y), envelope * jnp.sin(phase_y)], axis=2)
    left_table = left_table.reshape(orient * quarter * 2, quarter).astype(jnp.bfloat16)
    phase_x = wave_x[:, None, None] * (-offset_grid)[None]
    real_part = envelope * jnp.cos(phase_x)
    imag_part = envelope * jnp.sin(phase_x)
    upper_half = jnp.concatenate([real_part, imag_part], axis=2)
    lower_half = jnp.concatenate([-imag_part, real_part], axis=2)
    right_table = jnp.concatenate([upper_half, lower_half], axis=1).astype(jnp.bfloat16)
    return (left_table, right_table)


def phase_terms(coeffs, per_frame):
    quarter = coeffs.shape[-1] // 2
    coeff_real = coeffs[..., :quarter].astype(jnp.float32)
    coeff_imag = coeffs[..., quarter:].astype(jnp.float32)
    ref_real = per_frame[..., :quarter].astype(jnp.float32)
    ref_imag = per_frame[..., quarter:].astype(jnp.float32)
    prod_real = coeff_real * ref_real + coeff_imag * ref_imag
    prod_imag = coeff_imag * ref_real - coeff_real * ref_imag
    phase_signal = (
        prod_imag / jnp.sqrt(prod_real * prod_real + prod_imag * prod_imag + 1.0)
    ).astype(jnp.bfloat16)
    amplitude = coeff_real * coeff_real + coeff_imag * coeff_imag
    return (phase_signal, amplitude)


def taps_matrix(band_taps, frame_count):
    frame_index = jnp.arange(frame_count, dtype=jnp.int32)
    lag_grid = frame_index[:, None] - frame_index[None, :]
    one_hot = (
        lag_grid[:, :, None] == jnp.arange(band_taps.shape[0], dtype=jnp.int32)[None, None, :]
    ).astype(jnp.float32)
    return jnp.einsum("tsk,k->ts", one_hot, band_taps.astype(jnp.float32)).astype(jnp.bfloat16)


def segment_refs(segments, ref_pick, segment_count):
    numbers = jnp.arange(segment_count, dtype=jnp.int32)
    starts = jnp.sum((segments[None, :] < numbers[:, None]).astype(jnp.int32), axis=1)
    counts = jnp.sum((segments[None, :] == numbers[:, None]).astype(jnp.int32), axis=1)
    return starts + ref_pick % counts


def body(video_frames, segments, ref_pick, band_taps):
    frames_here = video_frames.shape[0]
    down_matrix = make_down(IMG, QUART)
    left_table, right_table = gabor_tables(QUART, ORIENT)

    def reduce_frames(pictures):
        half_done = jnp.einsum(
            "nia,qa->niq", pictures, down_matrix, preferred_element_type=jnp.float32
        ).astype(jnp.bfloat16)
        return jnp.einsum(
            "qi,nik->nqk", down_matrix, half_done, preferred_element_type=jnp.float32
        ).astype(jnp.bfloat16)

    def filter_frames(reduced):
        stacked = jnp.einsum(
            "ra,nak->nrk", left_table, reduced, preferred_element_type=jnp.float32
        ).astype(jnp.bfloat16)
        stacked = stacked.reshape(reduced.shape[0], ORIENT, QUART, 2 * QUART)
        return jnp.einsum(
            "noya,oab->noyb", stacked, right_table, preferred_element_type=jnp.float32
        ).astype(jnp.bfloat16)

    small_own = reduce_frames(video_frames)
    coeff_own = filter_frames(small_own)
    ref_frames = segment_refs(segments, ref_pick, NSEG)
    gathered = []
    for segment in range(NSEG):
        root_index = ref_frames[segment] // frames_here
        local_index = ref_frames[segment] % frames_here
        payload = lax.dynamic_index_in_dim(video_frames, local_index, 0, keepdims=False)
        gathered.append(spread(payload, "frames", root_index))
    ref_coeff = filter_frames(reduce_frames(jnp.stack(gathered)))
    first_frame = lax.axis_index("frames") * frames_here
    own_ids = lax.dynamic_slice_in_dim(segments, first_frame, frames_here)
    select = (own_ids[:, None] == jnp.arange(NSEG, dtype=jnp.int32)[None, :]).astype(jnp.bfloat16)
    per_frame = jnp.dot(select, ref_coeff.reshape(NSEG, -1), preferred_element_type=jnp.float32)
    per_frame = per_frame.astype(jnp.bfloat16).reshape(coeff_own.shape)
    phase_signal, amplitude = phase_terms(coeff_own, per_frame)
    phase_signal = phase_signal.reshape(frames_here, ORIENT, QUART * QUART)
    pixel_rows = lax.all_to_all(phase_signal, "frames", split_axis=2, concat_axis=0, tiled=True)
    matrix = taps_matrix(band_taps, pixel_rows.shape[0])
    filtered = jnp.einsum(
        "ts,sop->top", matrix, pixel_rows, preferred_element_type=jnp.float32
    ).astype(jnp.bfloat16)
    filtered = lax.all_to_all(filtered, "frames", split_axis=0, concat_axis=2, tiled=True)
    filtered = filtered.reshape(frames_here, ORIENT, QUART, QUART).astype(jnp.float32)
    return jnp.sum(amplitude * filtered, axis=1) / (jnp.sum(amplitude, axis=1) + 1.0)


PICK_LIMIT = 4096
REACH = 32


def down_table():
    position = np.arange(QUART, dtype=np.float32)[:, None]
    columns = np.arange(IMG, dtype=np.float32)[None, :]
    offset = columns - np.float32(4.0) * position - np.float32(1.5)
    weight = np.exp(-offset * offset / np.float32(2.0 * blur_sigma * blur_sigma))
    return (weight / np.sum(weight, axis=1, keepdims=True)).astype(jnp.bfloat16)


def waves():
    angles = np.arange(ORIENT, dtype=np.float32) * np.float32(math.pi / ORIENT)
    return np.float32(wave_number) * np.cos(angles), np.float32(wave_number) * np.sin(angles)


def gabor_envelope(offset):
    return np.float32(gabor_gain) * np.exp(-offset * offset / np.float32(2.0 * gabor_sigma * gabor_sigma))


def left_window(rows):
    offset = (
        np.arange(rows + 2 * REACH, dtype=np.float32)[None, :]
        - REACH
        - np.arange(rows, dtype=np.float32)[:, None]
    )
    envelope = gabor_envelope(offset)
    phase = waves()[1][:, None, None] * offset[None]
    table = np.stack([envelope * np.cos(phase), envelope * np.sin(phase)], axis=1)
    return table.reshape(ORIENT * 2 * rows, -1).astype(jnp.bfloat16)


def right_tables():
    position = np.arange(QUART, dtype=np.float32)
    offset = position[:, None] - position[None, :]
    envelope = gabor_envelope(offset)
    phase = waves()[0][:, None, None] * offset[None]
    real, imag = envelope * np.cos(phase), envelope * np.sin(phase)
    upper = np.concatenate([real, imag], axis=2)
    lower = np.concatenate([-imag, real], axis=2)
    return np.stack([upper, lower], axis=1).astype(jnp.bfloat16)


PLANE = 4
PAIR = 2


def flip(number, bits):
    step = 1
    while step <= bits:
        if bits & step:
            number = number + step - 2 * step * ((number // step) % 2)
        step *= 2
    return number


def make_kernel(parts, here, rows):
    frames = parts * here
    planes = parts // PLANE
    window = rows + 2 * REACH
    pair_window = PAIR * rows + 2 * REACH
    plane_window = PLANE * rows + 2 * REACH
    total = frames * rows
    chunks = 2

    def kernel(
        segments, picks, taps, video_hbm, down_hbm, down_t_hbm, left, right_hbm, out_hbm,
        video, down, down_t, right, half, reduced, gathered, stacked, coeffs,
        phase, matrix, numer, denom, moved, landed, out,
        load_sem, store_sem, send_1, recv_1, send_2, recv_2, send_3, recv_3, send_b, recv_b,
    ):
        me = lax.axis_index("frames")
        plane, spot = me // PLANE, me % PLANE
        across, sibling = flip(spot, PAIR), flip(spot, 1)
        barrier = pltpu.get_barrier_semaphore()

        def peer(j):
            return lax.rem(me + j, parts)

        def piece(n, part):
            height = IMG // chunks
            where = pl.ds(part * height, height)
            return pltpu.make_async_copy(
                video_hbm.at[n, where], video.at[n, where], load_sem.at[3 + n * chunks + part]
            )

        load_down_t = pltpu.make_async_copy(down_t_hbm, down_t, load_sem.at[0])
        load_down = pltpu.make_async_copy(down_hbm, down, load_sem.at[1])
        load_right = pltpu.make_async_copy(right_hbm, right, load_sem.at[2])
        load_down_t.start()
        for n in range(here):
            for part in range(chunks):
                piece(n, part).start()
            if n == 0:
                load_down.start()
        load_right.start()

        @pl.loop(1, parts)
        def _(j):
            pl.semaphore_signal(barrier, inc=1, device_id={"frames": peer(j)})

        edge = jnp.zeros((here, REACH, QUART), jnp.bfloat16)
        reduced[:, :REACH, :] = edge
        reduced[:, REACH + QUART :, :] = edge

        def frame_of(j, where, n):
            return (flip(plane, j) * PLANE + where) * here + n

        def rows_of(j, n, first, size):
            if j == 0:
                start = pl.multiple_of((plane * PLANE + first) * rows, rows)
                return reduced.at[n, pl.ds(start, size), :]
            return gathered.at[frame_of(j, spot, n), pl.ds(pl.multiple_of(first * rows, rows), size), :]

        def copy_1(j, n):
            to = flip(plane, j)
            start = pl.multiple_of(to * PLANE * rows, rows)
            return pltpu.make_async_remote_copy(
                src_ref=reduced.at[n, pl.ds(start, plane_window), :],
                dst_ref=gathered.at[me * here + n],
                send_sem=send_1.at[j, n],
                recv_sem=recv_1.at[j, n],
                device_id={"frames": to * PLANE + spot},
            )

        def copy_2(j, n):
            first = across // PAIR * PAIR
            where = pl.ds(pl.multiple_of(first * rows, rows), pair_window)
            return pltpu.make_async_remote_copy(
                src_ref=rows_of(j, n, first, pair_window),
                dst_ref=gathered.at[frame_of(j, spot, n), where, :],
                send_sem=send_2.at[j, n],
                recv_sem=recv_2.at[j, n],
                device_id={"frames": plane * PLANE + across},
            )

        sibling_rows = pl.ds(pl.multiple_of(sibling * rows, rows), window)

        def copy_3(j, n):
            return pltpu.make_async_remote_copy(
                src_ref=rows_of(j, n, sibling, window),
                dst_ref=gathered.at[frame_of(j, spot, n), sibling_rows, :],
                send_sem=send_3.at[j, n],
                recv_sem=recv_3.at[j, n],
                device_id={"frames": plane * PLANE + sibling},
            )

        def copy_4(j, n):
            part = gathered.at[frame_of(j, across, n), sibling_rows, :]
            return pltpu.make_async_remote_copy(
                src_ref=part,
                dst_ref=part,
                send_sem=send_3.at[planes + j, n],
                recv_sem=recv_3.at[planes + j, n],
                device_id={"frames": plane * PLANE + sibling},
            )

        load_down_t.wait()
        for n in range(here):
            for part in range(chunks):
                piece(n, part).wait()
                where = slice(part * (IMG // chunks), (part + 1) * (IMG // chunks))
                half[n, where] = jnp.dot(
                    video[n, where], down_t[...], preferred_element_type=jnp.float32
                ).astype(jnp.bfloat16)
            if n == 0:
                load_down.wait()
            reduced[n, REACH : REACH + QUART, :] = jnp.dot(
                down[...], half[n], preferred_element_type=jnp.float32
            ).astype(jnp.bfloat16)
            if n == 0:
                pl.semaphore_wait(barrier, parts - 1)
            for j in range(1, planes):
                copy_1(j, n).start()
            copy_2(0, n).start()
            copy_3(0, n).start()

        lag = lax.broadcasted_iota(jnp.int32, (frames, frames), 0) - lax.broadcasted_iota(
            jnp.int32, (frames, frames), 1
        )
        toeplitz = jnp.zeros((frames, frames), jnp.float32)
        tap_row = taps[...].astype(jnp.float32)
        for k in range(min(taps.shape[1], frames)):
            toeplitz = jnp.where(lag == k, tap_row[:, k : k + 1], toeplitz)
        owner = lax.broadcasted_iota(jnp.int32, (total, frames), 0) // rows
        repeat = jnp.where(
            owner == lax.broadcasted_iota(jnp.int32, (total, frames), 1), 1.0, 0.0
        ).astype(jnp.bfloat16)
        tall = jnp.dot(
            repeat, toeplitz.astype(jnp.bfloat16), preferred_element_type=jnp.float32
        ).astype(jnp.bfloat16)
        wide = lax.dot_general(
            tall, repeat, (((1,), (1,)), ((), ())), preferred_element_type=jnp.float32
        )
        same = (
            lax.broadcasted_iota(jnp.int32, (total, total), 0) % rows
            == lax.broadcasted_iota(jnp.int32, (total, total), 1) % rows
        )
        matrix[...] = jnp.where(same, wide, 0.0).astype(jnp.bfloat16)

        def stack_one(t, block):
            stacked[t] = (
                jnp.dot(left[...], block, preferred_element_type=jnp.float32)
                .astype(jnp.bfloat16)
                .reshape(ORIENT * 2, rows, QUART)
            )

        own_rows = pl.ds(pl.multiple_of(spot * rows, rows), window)

        def stack_arrived(j, where):
            @pl.loop(0, here)
            def _(n):
                t = frame_of(j, where, n)
                stack_one(t, gathered[t, own_rows, :])

        def second(j):
            for n in range(here):
                copy_2(j, n).wait_recv()
                copy_4(j, n).start()
            stack_arrived(j, across)

        for n in range(here):
            stack_one(me * here + n, reduced[n, pl.ds(pl.multiple_of(me * rows, rows), window), :])
        for j in range(1, planes):
            for n in range(here):
                copy_1(j, n).wait_recv()
                copy_2(j, n).start()
                copy_3(j, n).start()
            stack_arrived(j, spot)
            second(j - 1)
        for j in range(planes):
            for n in range(here):
                copy_3(j, n).wait_recv()
            stack_arrived(j, sibling)
        second(planes - 1)
        for j in range(planes):
            for n in range(here):
                copy_4(j, n).wait_recv()
            stack_arrived(j, flip(across, 1))

        load_right.wait()
        step = frames // 4
        for o in range(ORIENT):
            for part in range(4):
                where = slice(part * step, (part + 1) * step)
                value = jnp.dot(
                    stacked[where, 2 * o].reshape(step * rows, QUART),
                    right[o, 0],
                    preferred_element_type=jnp.float32,
                ) + jnp.dot(
                    stacked[where, 2 * o + 1].reshape(step * rows, QUART),
                    right[o, 1],
                    preferred_element_type=jnp.float32,
                )
                coeffs[where, o] = value.astype(jnp.bfloat16).reshape(step, rows, 2 * QUART)

        counts = [jnp.int32(0)] * NSEG
        for t in range(frames):
            for s in range(NSEG):
                counts[s] = counts[s] + jnp.where(segments[t] == s, 1, 0)
        picked, first = [], jnp.int32(0)
        for s in range(NSEG):
            rest = picks[s]
            for bit in reversed(range((PICK_LIMIT - 1).bit_length())):
                rest = jnp.where(rest >= counts[s] * (1 << bit), rest - counts[s] * (1 << bit), rest)
            picked.append(first + rest)
            first = first + counts[s]

        @pl.loop(0, frames)
        def _(t):
            ref = picked[NSEG - 1]
            for s in range(NSEG - 1):
                ref = jnp.where(segments[t] == s, picked[s], ref)
            ones = coeffs[t].astype(jnp.float32)
            base = coeffs[ref].astype(jnp.float32)
            real, imag = ones[..., :QUART], ones[..., QUART:]
            ref_real, ref_imag = base[..., :QUART], base[..., QUART:]
            prod_real = real * ref_real + imag * ref_imag
            prod_imag = imag * ref_real - real * ref_imag
            signal = prod_imag * lax.rsqrt(prod_real * prod_real + prod_imag * prod_imag + 1.0)
            phase[:, t] = signal.astype(jnp.bfloat16)
            denom[t] = jnp.sum(real * real + imag * imag, axis=0) + 1.0

        for o in range(ORIENT):
            filtered = (
                jnp.dot(
                    matrix[...],
                    phase[o].reshape(total, QUART),
                    preferred_element_type=jnp.float32,
                )
                .astype(jnp.bfloat16)
                .astype(jnp.float32)
                .reshape(frames, rows, QUART)
            )
            real = coeffs[:, o, :, :QUART].astype(jnp.float32)
            imag = coeffs[:, o, :, QUART:].astype(jnp.float32)
            term = (real * real + imag * imag) * filtered
            if o == 0:
                numer[...] = term
            elif o < ORIENT - 1:
                numer[...] += term
            else:
                moved[...] = ((numer[...] + term) / denom[...]).astype(jnp.bfloat16)

        here_rows = pl.ds(pl.multiple_of(me * rows, rows), rows)

        def return_copy(j):
            to = peer(j)
            return pltpu.make_async_remote_copy(
                src_ref=moved.at[pl.ds(to * here, here)],
                dst_ref=landed.at[:, here_rows, :],
                send_sem=send_b.at[j],
                recv_sem=recv_b.at[j],
                device_id={"frames": to},
            )

        @pl.loop(1, parts)
        def _(j):
            return_copy(j).start()

        landed[:, here_rows, :] = moved[pl.ds(me * here, here)]

        for n in range(here):
            for j in range(planes):
                if j:
                    copy_1(j, n).wait_send()
                copy_2(j, n).wait_send()
                copy_3(j, n).wait_send()
                copy_4(j, n).wait_send()

        @pl.loop(1, parts)
        def _(j):
            return_copy(j).wait_recv()

        out[...] = landed[...].astype(jnp.float32)
        store = pltpu.make_async_copy(out, out_hbm, store_sem)
        store.start()

        @pl.loop(1, parts)
        def _(j):
            return_copy(j).wait_send()

        store.wait()

    bf16, f32, dma = jnp.bfloat16, jnp.float32, pltpu.SemaphoreType.DMA
    anywhere = pl.BlockSpec(memory_space=pl.ANY)
    vmem = pl.BlockSpec(memory_space=pltpu.VMEM)
    smem = pl.BlockSpec(memory_space=pltpu.SMEM)
    return pl.pallas_call(
        kernel,
        out_shape=jax.ShapeDtypeStruct((here, QUART, QUART), f32),
        in_specs=[smem, smem, vmem, anywhere, anywhere, anywhere, vmem, anywhere],
        out_specs=anywhere,
        scratch_shapes=[
            pltpu.VMEM((here, IMG, IMG), bf16),
            pltpu.VMEM((QUART, IMG), bf16),
            pltpu.VMEM((IMG, QUART), bf16),
            pltpu.VMEM((ORIENT, 2, QUART, 2 * QUART), bf16),
            pltpu.VMEM((here, IMG, QUART), bf16),
            pltpu.VMEM((here, QUART + 2 * REACH, QUART), bf16),
            pltpu.VMEM((frames, plane_window, QUART), bf16),
            pltpu.VMEM((frames, ORIENT * 2, rows, QUART), bf16),
            pltpu.VMEM((frames, ORIENT, rows, 2 * QUART), bf16),
            pltpu.VMEM((ORIENT, frames, rows, QUART), bf16),
            pltpu.VMEM((total, total), bf16),
            pltpu.VMEM((frames, rows, QUART), f32),
            pltpu.VMEM((frames, rows, QUART), f32),
            pltpu.VMEM((frames, rows, QUART), bf16),
            pltpu.VMEM((here, QUART, QUART), bf16),
            pltpu.VMEM((here, QUART, QUART), f32),
            dma((3 + here * chunks,)),
            dma,
            dma((planes, here)),
            dma((planes, here)),
            dma((planes, here)),
            dma((planes, here)),
            dma((2 * planes, here)),
            dma((2 * planes, here)),
            dma((parts,)),
            dma((parts,)),
        ],
        compiler_params=pltpu.CompilerParams(
            collective_id=0, has_side_effects=True, vmem_limit_bytes=60 * 1024 * 1024
        ),
    )


def kernel_body(parts, video_frames, segments, ref_pick, band_taps):
    here = video_frames.shape[0]
    rows = QUART // parts
    down = down_table()
    return make_kernel(parts, here, rows)(
        segments,
        ref_pick,
        band_taps[None, :],
        video_frames,
        jnp.asarray(down),
        jnp.asarray(np.ascontiguousarray(down.T)),
        jnp.asarray(left_window(rows)),
        jnp.asarray(right_tables()),
    )


def solution(mesh):
    parts = mesh.shape["frames"]
    if QUART % parts == 0 and (QUART // parts) % 16 == 0 and parts in (4, 8, 16):
        chosen = lambda *args: kernel_body(parts, *args)
    else:
        chosen = body
    in_specs = (P(("groups", "frames"), None, None), P("groups"), P("groups"), P())
    out_specs = P(("groups", "frames"), None, None)
    return jax.shard_map(chosen, mesh=mesh, in_specs=in_specs, out_specs=out_specs, check_vma=False)
```

```python
import math

import jax
import numpy as np
import jax.numpy as jnp
from jax import lax
from jax.experimental import pallas as pl
from jax.experimental.pallas import tpu as pltpu
from jax.sharding import PartitionSpec as P

IMG = 1024
ORIENT = 4
NSEG = 4
QUART = 256


blur_sigma = 2.0
gabor_sigma = 2.0
wave_number = math.pi / 2.0
gabor_gain = 2.0


def spread(x, axis, root):
    mine = lax.axis_index(axis) == root
    return lax.psum(jnp.where(mine, x, jnp.zeros_like(x)), axis)


def make_down(full_size, quarter):
    position = jnp.arange(quarter, dtype=jnp.float32)[:, None]
    columns = jnp.arange(full_size, dtype=jnp.float32)[None, :]
    offset_grid = columns - 4.0 * position - 1.5
    weight = jnp.exp(-offset_grid * offset_grid / (2.0 * blur_sigma * blur_sigma))
    return (weight / jnp.sum(weight, axis=1, keepdims=True)).astype(jnp.bfloat16)


def gabor_tables(quarter, orient):
    position = jnp.arange(quarter, dtype=jnp.float32)
    offset_grid = position[None, :] - position[:, None]
    envelope = gabor_gain * jnp.exp(-offset_grid * offset_grid / (2.0 * gabor_sigma * gabor_sigma))
    angles = jnp.arange(orient, dtype=jnp.float32) * (math.pi / orient)
    wave_x = wave_number * jnp.cos(angles)
    wave_y = wave_number * jnp.sin(angles)
    phase_y = wave_y[:, None, None] * offset_grid[None]
    left_table = jnp.stack([envelope * jnp.cos(phase_y), envelope * jnp.sin(phase_y)], axis=2)
    left_table = left_table.reshape(orient * quarter * 2, quarter).astype(jnp.bfloat16)
    phase_x = wave_x[:, None, None] * (-offset_grid)[None]
    real_part = envelope * jnp.cos(phase_x)
    imag_part = envelope * jnp.sin(phase_x)
    upper_half = jnp.concatenate([real_part, imag_part], axis=2)
    lower_half = jnp.concatenate([-imag_part, real_part], axis=2)
    right_table = jnp.concatenate([upper_half, lower_half], axis=1).astype(jnp.bfloat16)
    return (left_table, right_table)


def phase_terms(coeffs, per_frame):
    quarter = coeffs.shape[-1] // 2
    coeff_real = coeffs[..., :quarter].astype(jnp.float32)
    coeff_imag = coeffs[..., quarter:].astype(jnp.float32)
    ref_real = per_frame[..., :quarter].astype(jnp.float32)
    ref_imag = per_frame[..., quarter:].astype(jnp.float32)
    prod_real = coeff_real * ref_real + coeff_imag * ref_imag
    prod_imag = coeff_imag * ref_real - coeff_real * ref_imag
    phase_signal = (
        prod_imag / jnp.sqrt(prod_real * prod_real + prod_imag * prod_imag + 1.0)
    ).astype(jnp.bfloat16)
    amplitude = coeff_real * coeff_real + coeff_imag * coeff_imag
    return (phase_signal, amplitude)


def taps_matrix(band_taps, frame_count):
    frame_index = jnp.arange(frame_count, dtype=jnp.int32)
    lag_grid = frame_index[:, None] - frame_index[None, :]
    one_hot = (
        lag_grid[:, :, None] == jnp.arange(band_taps.shape[0], dtype=jnp.int32)[None, None, :]
    ).astype(jnp.float32)
    return jnp.einsum("tsk,k->ts", one_hot, band_taps.astype(jnp.float32)).astype(jnp.bfloat16)


def segment_refs(segments, ref_pick, segment_count):
    numbers = jnp.arange(segment_count, dtype=jnp.int32)
    starts = jnp.sum((segments[None, :] < numbers[:, None]).astype(jnp.int32), axis=1)
    counts = jnp.sum((segments[None, :] == numbers[:, None]).astype(jnp.int32), axis=1)
    return starts + ref_pick % counts


def body(video_frames, segments, ref_pick, band_taps):
    frames_here = video_frames.shape[0]
    down_matrix = make_down(IMG, QUART)
    left_table, right_table = gabor_tables(QUART, ORIENT)

    def reduce_frames(pictures):
        half_done = jnp.einsum(
            "nia,qa->niq", pictures, down_matrix, preferred_element_type=jnp.float32
        ).astype(jnp.bfloat16)
        return jnp.einsum(
            "qi,nik->nqk", down_matrix, half_done, preferred_element_type=jnp.float32
        ).astype(jnp.bfloat16)

    def filter_frames(reduced):
        stacked = jnp.einsum(
            "ra,nak->nrk", left_table, reduced, preferred_element_type=jnp.float32
        ).astype(jnp.bfloat16)
        stacked = stacked.reshape(reduced.shape[0], ORIENT, QUART, 2 * QUART)
        return jnp.einsum(
            "noya,oab->noyb", stacked, right_table, preferred_element_type=jnp.float32
        ).astype(jnp.bfloat16)

    small_own = reduce_frames(video_frames)
    coeff_own = filter_frames(small_own)
    ref_frames = segment_refs(segments, ref_pick, NSEG)
    gathered = []
    for segment in range(NSEG):
        root_index = ref_frames[segment] // frames_here
        local_index = ref_frames[segment] % frames_here
        payload = lax.dynamic_index_in_dim(video_frames, local_index, 0, keepdims=False)
        gathered.append(spread(payload, "frames", root_index))
    ref_coeff = filter_frames(reduce_frames(jnp.stack(gathered)))
    first_frame = lax.axis_index("frames") * frames_here
    own_ids = lax.dynamic_slice_in_dim(segments, first_frame, frames_here)
    select = (own_ids[:, None] == jnp.arange(NSEG, dtype=jnp.int32)[None, :]).astype(jnp.bfloat16)
    per_frame = jnp.dot(select, ref_coeff.reshape(NSEG, -1), preferred_element_type=jnp.float32)
    per_frame = per_frame.astype(jnp.bfloat16).reshape(coeff_own.shape)
    phase_signal, amplitude = phase_terms(coeff_own, per_frame)
    phase_signal = phase_signal.reshape(frames_here, ORIENT, QUART * QUART)
    pixel_rows = lax.all_to_all(phase_signal, "frames", split_axis=2, concat_axis=0, tiled=True)
    matrix = taps_matrix(band_taps, pixel_rows.shape[0])
    filtered = jnp.einsum(
        "ts,sop->top", matrix, pixel_rows, preferred_element_type=jnp.float32
    ).astype(jnp.bfloat16)
    filtered = lax.all_to_all(filtered, "frames", split_axis=0, concat_axis=2, tiled=True)
    filtered = filtered.reshape(frames_here, ORIENT, QUART, QUART).astype(jnp.float32)
    return jnp.sum(amplitude * filtered, axis=1) / (jnp.sum(amplitude, axis=1) + 1.0)


PICK_LIMIT = 4096
REACH = 32


def down_table():
    position = np.arange(QUART, dtype=np.float32)[:, None]
    columns = np.arange(IMG, dtype=np.float32)[None, :]
    offset = columns - np.float32(4.0) * position - np.float32(1.5)
    weight = np.exp(-offset * offset / np.float32(2.0 * blur_sigma * blur_sigma))
    return (weight / np.sum(weight, axis=1, keepdims=True)).astype(jnp.bfloat16)


def waves():
    angles = np.arange(ORIENT, dtype=np.float32) * np.float32(math.pi / ORIENT)
    return np.float32(wave_number) * np.cos(angles), np.float32(wave_number) * np.sin(angles)


def gabor_envelope(offset):
    return np.float32(gabor_gain) * np.exp(-offset * offset / np.float32(2.0 * gabor_sigma * gabor_sigma))


def left_window(rows):
    offset = (
        np.arange(rows + 2 * REACH, dtype=np.float32)[None, :]
        - REACH
        - np.arange(rows, dtype=np.float32)[:, None]
    )
    envelope = gabor_envelope(offset)
    phase = waves()[1][:, None, None] * offset[None]
    table = np.stack([envelope * np.cos(phase), envelope * np.sin(phase)], axis=1)
    return table.reshape(ORIENT * 2 * rows, -1).astype(jnp.bfloat16)


def right_tables():
    position = np.arange(QUART, dtype=np.float32)
    offset = position[:, None] - position[None, :]
    envelope = gabor_envelope(offset)
    phase = waves()[0][:, None, None] * offset[None]
    real, imag = envelope * np.cos(phase), envelope * np.sin(phase)
    upper = np.concatenate([real, imag], axis=2)
    lower = np.concatenate([-imag, real], axis=2)
    return np.stack([upper, lower], axis=1).astype(jnp.bfloat16)


PLANE = 4
PAIR = 2


def flip(number, bits):
    step = 1
    while step <= bits:
        if bits & step:
            number = number + step - 2 * step * ((number // step) % 2)
        step *= 2
    return number


def make_kernel(parts, here, rows):
    frames = parts * here
    planes = parts // PLANE
    window = rows + 2 * REACH
    pair_window = PAIR * rows + 2 * REACH
    plane_window = PLANE * rows + 2 * REACH
    total = frames * rows
    chunks = 2

    def kernel(
        segments, picks, taps, video_hbm, down_hbm, down_t_hbm, left, right_hbm, out_hbm,
        video, down, down_t, right, half, reduced, gathered, stacked, coeffs,
        phase, matrix, numer, denom, moved,
        load_sem, store_sem, send_1, recv_1, send_2, recv_2, send_3, recv_3, send_b, recv_b,
    ):
        me = lax.axis_index("frames")
        plane, spot = me // PLANE, me % PLANE
        across, sibling = flip(spot, PAIR), flip(spot, 1)
        barrier = pltpu.get_barrier_semaphore()

        def peer(j):
            return lax.rem(me + j, parts)

        def piece(n, part):
            height = IMG // chunks
            where = pl.ds(part * height, height)
            return pltpu.make_async_copy(
                video_hbm.at[n, where], video.at[n, where], load_sem.at[3 + n * chunks + part]
            )

        load_down_t = pltpu.make_async_copy(down_t_hbm, down_t, load_sem.at[0])
        load_down = pltpu.make_async_copy(down_hbm, down, load_sem.at[1])
        load_right = pltpu.make_async_copy(right_hbm, right, load_sem.at[2])
        load_down_t.start()
        for n in range(here):
            for part in range(chunks):
                piece(n, part).start()
            if n == 0:
                load_down.start()
        load_right.start()

        blank = jnp.zeros((frames, REACH, QUART), jnp.bfloat16)

        @pl.when(plane == 0)
        def _():
            gathered[:, :REACH, :] = blank

        @pl.when(plane == planes - 1)
        def _():
            gathered[:, plane_window - REACH :, :] = blank

        @pl.loop(1, parts)
        def _(j):
            pl.semaphore_signal(barrier, inc=1, device_id={"frames": peer(j)})

        edge = jnp.zeros((here, REACH, QUART), jnp.bfloat16)
        reduced[:, :REACH, :] = edge
        reduced[:, REACH + QUART :, :] = edge

        def frame_of(j, where, n):
            return (flip(plane, j) * PLANE + where) * here + n

        def rows_of(j, n, first, size):
            if j == 0:
                start = pl.multiple_of((plane * PLANE + first) * rows, rows)
                return reduced.at[n, pl.ds(start, size), :]
            return gathered.at[frame_of(j, spot, n), pl.ds(pl.multiple_of(first * rows, rows), size), :]

        def copy_1(j, n, low, high):
            to = flip(plane, j)
            start = pl.multiple_of(to * PLANE * rows + low, rows)
            return pltpu.make_async_remote_copy(
                src_ref=reduced.at[n, pl.ds(start, high - low), :],
                dst_ref=gathered.at[me * here + n, pl.ds(low, high - low), :],
                send_sem=send_1.at[j, n],
                recv_sem=recv_1.at[j, n],
                device_id={"frames": to * PLANE + spot},
            )

        def each_1(j, n, to, act):
            @pl.when(to == 0)
            def _():
                act(copy_1(j, n, REACH, plane_window))

            @pl.when(to == planes - 1)
            def _():
                act(copy_1(j, n, 0, plane_window - REACH))

            if planes > 2:

                @pl.when((to > 0) & (to < planes - 1))
                def _():
                    act(copy_1(j, n, 0, plane_window))

        def copy_2(j, n):
            first = across // PAIR * PAIR
            where = pl.ds(pl.multiple_of(first * rows, rows), pair_window)
            return pltpu.make_async_remote_copy(
                src_ref=rows_of(j, n, first, pair_window),
                dst_ref=gathered.at[frame_of(j, spot, n), where, :],
                send_sem=send_2.at[j, n],
                recv_sem=recv_2.at[j, n],
                device_id={"frames": plane * PLANE + across},
            )

        sibling_rows = pl.ds(pl.multiple_of(sibling * rows, rows), window)

        def copy_3(j, n):
            return pltpu.make_async_remote_copy(
                src_ref=rows_of(j, n, sibling, window),
                dst_ref=gathered.at[frame_of(j, spot, n), sibling_rows, :],
                send_sem=send_3.at[j, n],
                recv_sem=recv_3.at[j, n],
                device_id={"frames": plane * PLANE + sibling},
            )

        def copy_4(j, n):
            part = gathered.at[frame_of(j, across, n), sibling_rows, :]
            return pltpu.make_async_remote_copy(
                src_ref=part,
                dst_ref=part,
                send_sem=send_3.at[planes + j, n],
                recv_sem=recv_3.at[planes + j, n],
                device_id={"frames": plane * PLANE + sibling},
            )

        load_down_t.wait()
        for n in range(here):
            for part in range(chunks):
                piece(n, part).wait()
                where = slice(part * (IMG // chunks), (part + 1) * (IMG // chunks))
                half[n, where] = jnp.dot(
                    video[n, where], down_t[...], preferred_element_type=jnp.float32
                ).astype(jnp.bfloat16)
            if n == 0:
                load_down.wait()
            reduced[n, REACH : REACH + QUART, :] = jnp.dot(
                down[...], half[n], preferred_element_type=jnp.float32
            ).astype(jnp.bfloat16)
            if n == 0:
                pl.semaphore_wait(barrier, parts - 1)
            for j in range(1, planes):
                each_1(j, n, flip(plane, j), lambda copy: copy.start())
            copy_2(0, n).start()
            copy_3(0, n).start()

        lag = lax.broadcasted_iota(jnp.int32, (frames, frames), 0) - lax.broadcasted_iota(
            jnp.int32, (frames, frames), 1
        )
        toeplitz = jnp.zeros((frames, frames), jnp.float32)
        tap_row = taps[...].astype(jnp.float32)
        for k in range(min(taps.shape[1], frames)):
            toeplitz = jnp.where(lag == k, tap_row[:, k : k + 1], toeplitz)
        owner = lax.broadcasted_iota(jnp.int32, (total, frames), 0) // rows
        repeat = jnp.where(
            owner == lax.broadcasted_iota(jnp.int32, (total, frames), 1), 1.0, 0.0
        ).astype(jnp.bfloat16)
        tall = jnp.dot(
            repeat, toeplitz.astype(jnp.bfloat16), preferred_element_type=jnp.float32
        ).astype(jnp.bfloat16)
        wide = lax.dot_general(
            tall, repeat, (((1,), (1,)), ((), ())), preferred_element_type=jnp.float32
        )
        same = (
            lax.broadcasted_iota(jnp.int32, (total, total), 0) % rows
            == lax.broadcasted_iota(jnp.int32, (total, total), 1) % rows
        )
        matrix[...] = jnp.where(same, wide, 0.0).astype(jnp.bfloat16)

        def stack_one(place, block):
            stacked[place] = (
                jnp.dot(left[...], block, preferred_element_type=jnp.float32)
                .astype(jnp.bfloat16)
                .reshape(ORIENT * 2, rows, QUART)
            )

        def coefficients(where):
            for o in range(ORIENT):
                value = jnp.dot(
                    stacked[:, where, :, 2 * o].reshape(planes * here * rows, QUART),
                    right[o, 0],
                    preferred_element_type=jnp.float32,
                ) + jnp.dot(
                    stacked[:, where, :, 2 * o + 1].reshape(planes * here * rows, QUART),
                    right[o, 1],
                    preferred_element_type=jnp.float32,
                )
                value = value.astype(jnp.bfloat16).reshape(planes, here, rows, 2 * QUART)
                for p in range(planes):
                    coeffs[pl.ds((p * PLANE + where) * here, here), o] = value[p]

        own_rows = pl.ds(pl.multiple_of(spot * rows, rows), window)

        def stack_arrived(j, where):
            @pl.loop(0, here)
            def _(n):
                t = frame_of(j, where, n)
                stack_one((flip(plane, j), where, n), gathered[t, own_rows, :])

        def second(j):
            for n in range(here):
                copy_2(j, n).wait_recv()
                copy_4(j, n).start()
            stack_arrived(j, across)

        for n in range(here):
            stack_one((plane, spot, n), reduced[n, pl.ds(pl.multiple_of(me * rows, rows), window), :])
        for j in range(1, planes):
            for n in range(here):
                each_1(j, n, plane, lambda copy: copy.wait_recv())
                copy_2(j, n).start()
                copy_3(j, n).start()
            stack_arrived(j, spot)
            second(j - 1)
        load_right.wait()
        coefficients(spot)
        second(planes - 1)
        for j in range(planes):
            for n in range(here):
                copy_3(j, n).wait_recv()
            stack_arrived(j, sibling)
        coefficients(across)
        coefficients(sibling)
        last = flip(across, 1)
        for j in range(planes):
            for n in range(here):
                copy_4(j, n).wait_recv()
            stack_arrived(j, last)
        coefficients(last)

        counts = [jnp.int32(0)] * NSEG
        for t in range(frames):
            for s in range(NSEG):
                counts[s] = counts[s] + jnp.where(segments[t] == s, 1, 0)
        picked, first = [], jnp.int32(0)
        for s in range(NSEG):
            rest = picks[s]
            for bit in reversed(range((PICK_LIMIT - 1).bit_length())):
                rest = jnp.where(rest >= counts[s] * (1 << bit), rest - counts[s] * (1 << bit), rest)
            picked.append(first + rest)
            first = first + counts[s]

        @pl.loop(0, frames)
        def _(t):
            ref = picked[NSEG - 1]
            for s in range(NSEG - 1):
                ref = jnp.where(segments[t] == s, picked[s], ref)
            ones = coeffs[t].astype(jnp.float32)
            base = coeffs[ref].astype(jnp.float32)
            real, imag = ones[..., :QUART], ones[..., QUART:]
            ref_real, ref_imag = base[..., :QUART], base[..., QUART:]
            prod_real = real * ref_real + imag * ref_imag
            prod_imag = imag * ref_real - real * ref_imag
            signal = prod_imag * lax.rsqrt(prod_real * prod_real + prod_imag * prod_imag + 1.0)
            phase[:, t] = signal.astype(jnp.bfloat16)
            denom[t] = jnp.sum(real * real + imag * imag, axis=0) + 1.0

        here_rows = pl.ds(pl.multiple_of(me * rows, rows), rows)

        def return_copy(j):
            to = peer(j)
            return pltpu.make_async_remote_copy(
                src_ref=moved.at[pl.ds(to * here, here)],
                dst_ref=out_hbm.at[:, here_rows, :],
                send_sem=send_b.at[j],
                recv_sem=recv_b.at[j],
                device_id={"frames": to},
            )

        crowd = parts // 2
        near = me // crowd

        def filter_half(number):
            span = pl.ds(number * (frames // 2), frames // 2)
            long_span = pl.ds(pl.multiple_of(number * (total // 2), total // 2), total // 2)
            for o in range(ORIENT):
                filtered = (
                    jnp.dot(
                        matrix[long_span, :],
                        phase[o].reshape(total, QUART),
                        preferred_element_type=jnp.float32,
                    )
                    .astype(jnp.bfloat16)
                    .astype(jnp.float32)
                    .reshape(frames // 2, rows, QUART)
                )
                real = coeffs[span, o, :, :QUART].astype(jnp.float32)
                imag = coeffs[span, o, :, QUART:].astype(jnp.float32)
                term = (real * real + imag * imag) * filtered
                if o == 0:
                    numer[...] = term
                elif o < ORIENT - 1:
                    numer[...] += term
                else:
                    moved[span] = ((numer[...] + term) / denom[span]).astype(jnp.bfloat16)

        filter_half(1 - near)

        @pl.loop(0, crowd)
        def _(k):
            to = (1 - near) * crowd + lax.rem(me + k, crowd)
            return_copy(lax.rem(to + parts - me, parts)).start()

        filter_half(near)

        @pl.loop(1, crowd)
        def _(k):
            to = near * crowd + lax.rem(me + k, crowd)
            return_copy(lax.rem(to + parts - me, parts)).start()

        store = pltpu.make_async_copy(
            moved.at[pl.ds(me * here, here)], out_hbm.at[:, here_rows, :], store_sem
        )
        store.start()

        for n in range(here):
            for j in range(planes):
                if j:
                    each_1(j, n, flip(plane, j), lambda copy: copy.wait_send())
                copy_2(j, n).wait_send()
                copy_3(j, n).wait_send()
                copy_4(j, n).wait_send()

        @pl.loop(1, parts)
        def _(j):
            return_copy(j).wait_recv()

        @pl.loop(1, parts)
        def _(j):
            return_copy(j).wait_send()

        store.wait()

    bf16, f32, dma = jnp.bfloat16, jnp.float32, pltpu.SemaphoreType.DMA
    anywhere = pl.BlockSpec(memory_space=pl.ANY)
    vmem = pl.BlockSpec(memory_space=pltpu.VMEM)
    smem = pl.BlockSpec(memory_space=pltpu.SMEM)
    return pl.pallas_call(
        kernel,
        out_shape=jax.ShapeDtypeStruct((here, QUART, QUART), bf16),
        in_specs=[smem, smem, vmem, anywhere, anywhere, anywhere, vmem, anywhere],
        out_specs=anywhere,
        scratch_shapes=[
            pltpu.VMEM((here, IMG, IMG), bf16),
            pltpu.VMEM((QUART, IMG), bf16),
            pltpu.VMEM((IMG, QUART), bf16),
            pltpu.VMEM((ORIENT, 2, QUART, 2 * QUART), bf16),
            pltpu.VMEM((here, IMG, QUART), bf16),
            pltpu.VMEM((here, QUART + 2 * REACH, QUART), bf16),
            pltpu.VMEM((frames, plane_window, QUART), bf16),
            pltpu.VMEM((planes, PLANE, here, ORIENT * 2, rows, QUART), bf16),
            pltpu.VMEM((frames, ORIENT, rows, 2 * QUART), bf16),
            pltpu.VMEM((ORIENT, frames, rows, QUART), bf16),
            pltpu.VMEM((total, total), bf16),
            pltpu.VMEM((frames // 2, rows, QUART), f32),
            pltpu.VMEM((frames, rows, QUART), f32),
            pltpu.VMEM((frames, rows, QUART), bf16),
            dma((3 + here * chunks,)),
            dma,
            dma((planes, here)),
            dma((planes, here)),
            dma((planes, here)),
            dma((planes, here)),
            dma((2 * planes, here)),
            dma((2 * planes, here)),
            dma((parts,)),
            dma((parts,)),
        ],
        compiler_params=pltpu.CompilerParams(
            collective_id=0, has_side_effects=True, vmem_limit_bytes=60 * 1024 * 1024
        ),
    )


def kernel_body(parts, video_frames, segments, ref_pick, band_taps):
    here = video_frames.shape[0]
    rows = QUART // parts
    down = down_table()
    return make_kernel(parts, here, rows)(
        segments,
        ref_pick,
        band_taps[None, :],
        video_frames,
        jnp.asarray(down),
        jnp.asarray(np.ascontiguousarray(down.T)),
        jnp.asarray(left_window(rows)),
        jnp.asarray(right_tables()),
    ).astype(jnp.float32)


def solution(mesh):
    parts = mesh.shape["frames"]
    if QUART % parts == 0 and (QUART // parts) % 16 == 0 and parts in (4, 8, 16):
        chosen = lambda *args: kernel_body(parts, *args)
    else:
        chosen = body
    in_specs = (P(("groups", "frames"), None, None), P("groups"), P("groups"), P())
    out_specs = P(("groups", "frames"), None, None)
    return jax.shard_map(chosen, mesh=mesh, in_specs=in_specs, out_specs=out_specs, check_vma=False)
```

```python
import math

import jax
import numpy as np
import jax.numpy as jnp
from jax import lax
from jax.experimental import pallas as pl
from jax.experimental.pallas import tpu as pltpu
from jax.sharding import PartitionSpec as P

IMG = 1024
ORIENT = 4
NSEG = 4
QUART = 256


blur_sigma = 2.0
gabor_sigma = 2.0
wave_number = math.pi / 2.0
gabor_gain = 2.0


def spread(x, axis, root):
    mine = lax.axis_index(axis) == root
    return lax.psum(jnp.where(mine, x, jnp.zeros_like(x)), axis)


def make_down(full_size, quarter):
    position = jnp.arange(quarter, dtype=jnp.float32)[:, None]
    columns = jnp.arange(full_size, dtype=jnp.float32)[None, :]
    offset_grid = columns - 4.0 * position - 1.5
    weight = jnp.exp(-offset_grid * offset_grid / (2.0 * blur_sigma * blur_sigma))
    return (weight / jnp.sum(weight, axis=1, keepdims=True)).astype(jnp.bfloat16)


def gabor_tables(quarter, orient):
    position = jnp.arange(quarter, dtype=jnp.float32)
    offset_grid = position[None, :] - position[:, None]
    envelope = gabor_gain * jnp.exp(-offset_grid * offset_grid / (2.0 * gabor_sigma * gabor_sigma))
    angles = jnp.arange(orient, dtype=jnp.float32) * (math.pi / orient)
    wave_x = wave_number * jnp.cos(angles)
    wave_y = wave_number * jnp.sin(angles)
    phase_y = wave_y[:, None, None] * offset_grid[None]
    left_table = jnp.stack([envelope * jnp.cos(phase_y), envelope * jnp.sin(phase_y)], axis=2)
    left_table = left_table.reshape(orient * quarter * 2, quarter).astype(jnp.bfloat16)
    phase_x = wave_x[:, None, None] * (-offset_grid)[None]
    real_part = envelope * jnp.cos(phase_x)
    imag_part = envelope * jnp.sin(phase_x)
    upper_half = jnp.concatenate([real_part, imag_part], axis=2)
    lower_half = jnp.concatenate([-imag_part, real_part], axis=2)
    right_table = jnp.concatenate([upper_half, lower_half], axis=1).astype(jnp.bfloat16)
    return (left_table, right_table)


def phase_terms(coeffs, per_frame):
    quarter = coeffs.shape[-1] // 2
    coeff_real = coeffs[..., :quarter].astype(jnp.float32)
    coeff_imag = coeffs[..., quarter:].astype(jnp.float32)
    ref_real = per_frame[..., :quarter].astype(jnp.float32)
    ref_imag = per_frame[..., quarter:].astype(jnp.float32)
    prod_real = coeff_real * ref_real + coeff_imag * ref_imag
    prod_imag = coeff_imag * ref_real - coeff_real * ref_imag
    phase_signal = (
        prod_imag / jnp.sqrt(prod_real * prod_real + prod_imag * prod_imag + 1.0)
    ).astype(jnp.bfloat16)
    amplitude = coeff_real * coeff_real + coeff_imag * coeff_imag
    return (phase_signal, amplitude)


def taps_matrix(band_taps, frame_count):
    frame_index = jnp.arange(frame_count, dtype=jnp.int32)
    lag_grid = frame_index[:, None] - frame_index[None, :]
    one_hot = (
        lag_grid[:, :, None] == jnp.arange(band_taps.shape[0], dtype=jnp.int32)[None, None, :]
    ).astype(jnp.float32)
    return jnp.einsum("tsk,k->ts", one_hot, band_taps.astype(jnp.float32)).astype(jnp.bfloat16)


def segment_refs(segments, ref_pick, segment_count):
    numbers = jnp.arange(segment_count, dtype=jnp.int32)
    starts = jnp.sum((segments[None, :] < numbers[:, None]).astype(jnp.int32), axis=1)
    counts = jnp.sum((segments[None, :] == numbers[:, None]).astype(jnp.int32), axis=1)
    return starts + ref_pick % counts


def body(video_frames, segments, ref_pick, band_taps):
    frames_here = video_frames.shape[0]
    down_matrix = make_down(IMG, QUART)
    left_table, right_table = gabor_tables(QUART, ORIENT)

    def reduce_frames(pictures):
        half_done = jnp.einsum(
            "nia,qa->niq", pictures, down_matrix, preferred_element_type=jnp.float32
        ).astype(jnp.bfloat16)
        return jnp.einsum(
            "qi,nik->nqk", down_matrix, half_done, preferred_element_type=jnp.float32
        ).astype(jnp.bfloat16)

    def filter_frames(reduced):
        stacked = jnp.einsum(
            "ra,nak->nrk", left_table, reduced, preferred_element_type=jnp.float32
        ).astype(jnp.bfloat16)
        stacked = stacked.reshape(reduced.shape[0], ORIENT, QUART, 2 * QUART)
        return jnp.einsum(
            "noya,oab->noyb", stacked, right_table, preferred_element_type=jnp.float32
        ).astype(jnp.bfloat16)

    small_own = reduce_frames(video_frames)
    coeff_own = filter_frames(small_own)
    ref_frames = segment_refs(segments, ref_pick, NSEG)
    gathered = []
    for segment in range(NSEG):
        root_index = ref_frames[segment] // frames_here
        local_index = ref_frames[segment] % frames_here
        payload = lax.dynamic_index_in_dim(video_frames, local_index, 0, keepdims=False)
        gathered.append(spread(payload, "frames", root_index))
    ref_coeff = filter_frames(reduce_frames(jnp.stack(gathered)))
    first_frame = lax.axis_index("frames") * frames_here
    own_ids = lax.dynamic_slice_in_dim(segments, first_frame, frames_here)
    select = (own_ids[:, None] == jnp.arange(NSEG, dtype=jnp.int32)[None, :]).astype(jnp.bfloat16)
    per_frame = jnp.dot(select, ref_coeff.reshape(NSEG, -1), preferred_element_type=jnp.float32)
    per_frame = per_frame.astype(jnp.bfloat16).reshape(coeff_own.shape)
    phase_signal, amplitude = phase_terms(coeff_own, per_frame)
    phase_signal = phase_signal.reshape(frames_here, ORIENT, QUART * QUART)
    pixel_rows = lax.all_to_all(phase_signal, "frames", split_axis=2, concat_axis=0, tiled=True)
    matrix = taps_matrix(band_taps, pixel_rows.shape[0])
    filtered = jnp.einsum(
        "ts,sop->top", matrix, pixel_rows, preferred_element_type=jnp.float32
    ).astype(jnp.bfloat16)
    filtered = lax.all_to_all(filtered, "frames", split_axis=0, concat_axis=2, tiled=True)
    filtered = filtered.reshape(frames_here, ORIENT, QUART, QUART).astype(jnp.float32)
    return jnp.sum(amplitude * filtered, axis=1) / (jnp.sum(amplitude, axis=1) + 1.0)


PICK_LIMIT = 4096
REACH = 32


def down_table():
    position = np.arange(QUART, dtype=np.float32)[:, None]
    columns = np.arange(IMG, dtype=np.float32)[None, :]
    offset = columns - np.float32(4.0) * position - np.float32(1.5)
    weight = np.exp(-offset * offset / np.float32(2.0 * blur_sigma * blur_sigma))
    return (weight / np.sum(weight, axis=1, keepdims=True)).astype(jnp.bfloat16)


def waves():
    angles = np.arange(ORIENT, dtype=np.float32) * np.float32(math.pi / ORIENT)
    return np.float32(wave_number) * np.cos(angles), np.float32(wave_number) * np.sin(angles)


def gabor_envelope(offset):
    return np.float32(gabor_gain) * np.exp(-offset * offset / np.float32(2.0 * gabor_sigma * gabor_sigma))


def left_window(rows):
    offset = (
        np.arange(rows + 2 * REACH, dtype=np.float32)[None, :]
        - REACH
        - np.arange(rows, dtype=np.float32)[:, None]
    )
    envelope = gabor_envelope(offset)
    phase = waves()[1][:, None, None] * offset[None]
    table = np.stack([envelope * np.cos(phase), envelope * np.sin(phase)], axis=1)
    return table.reshape(ORIENT * 2 * rows, -1).astype(jnp.bfloat16)


def right_tables():
    position = np.arange(QUART, dtype=np.float32)
    offset = position[:, None] - position[None, :]
    envelope = gabor_envelope(offset)
    phase = waves()[0][:, None, None] * offset[None]
    real, imag = envelope * np.cos(phase), envelope * np.sin(phase)
    upper = np.concatenate([real, imag], axis=2)
    lower = np.concatenate([-imag, real], axis=2)
    return np.stack([upper, lower], axis=1).astype(jnp.bfloat16)


PLANE = 4
PAIR = 2


def flip(number, bits):
    step = 1
    while step <= bits:
        if bits & step:
            number = number + step - 2 * step * ((number // step) % 2)
        step *= 2
    return number


def make_kernel(parts, here, rows):
    frames = parts * here
    planes = parts // PLANE
    window = rows + 2 * REACH
    pair_window = PAIR * rows + 2 * REACH
    plane_window = PLANE * rows + 2 * REACH
    total = frames * rows
    chunks = 2

    def kernel(
        segments, picks, taps, video_hbm, down_hbm, down_t_hbm, left, right_hbm, out_hbm,
        video, down, down_t, right, half, reduced, gathered, stacked, coeffs,
        phase, matrix, numer, denom, moved,
        load_sem, store_sem, send_1, recv_1, send_2, recv_2, send_3, recv_3, send_b, recv_b,
    ):
        me = lax.axis_index("frames")
        plane, spot = me // PLANE, me % PLANE
        across, sibling = flip(spot, PAIR), flip(spot, 1)
        barrier = pltpu.get_barrier_semaphore()

        def peer(j):
            return lax.rem(me + j, parts)

        def piece(n, part):
            height = IMG // chunks
            where = pl.ds(part * height, height)
            return pltpu.make_async_copy(
                video_hbm.at[n, where], video.at[n, where], load_sem.at[3 + n * chunks + part]
            )

        load_down_t = pltpu.make_async_copy(down_t_hbm, down_t, load_sem.at[0])
        load_down = pltpu.make_async_copy(down_hbm, down, load_sem.at[1])
        load_right = pltpu.make_async_copy(right_hbm, right, load_sem.at[2])
        load_down_t.start()
        for n in range(here):
            for part in range(chunks):
                piece(n, part).start()
            if n == 0:
                load_down.start()
        load_right.start()

        blank = jnp.zeros((frames, REACH, QUART), jnp.bfloat16)

        @pl.when(plane == 0)
        def _():
            gathered[:, :REACH, :] = blank

        @pl.when(plane == planes - 1)
        def _():
            gathered[:, plane_window - REACH :, :] = blank

        @pl.loop(1, parts)
        def _(j):
            pl.semaphore_signal(barrier, inc=1, device_id={"frames": peer(j)})

        edge = jnp.zeros((here, REACH, QUART), jnp.bfloat16)
        reduced[:, :REACH, :] = edge
        reduced[:, REACH + QUART :, :] = edge

        def frame_of(j, where, n):
            return (flip(plane, j) * PLANE + where) * here + n

        def rows_of(j, n, first, size):
            if j == 0:
                start = pl.multiple_of((plane * PLANE + first) * rows, rows)
                return reduced.at[n, pl.ds(start, size), :]
            return gathered.at[frame_of(j, spot, n), pl.ds(pl.multiple_of(first * rows, rows), size), :]

        def copy_1(j, n, low, high):
            to = flip(plane, j)
            start = pl.multiple_of(to * PLANE * rows + low, rows)
            return pltpu.make_async_remote_copy(
                src_ref=reduced.at[n, pl.ds(start, high - low), :],
                dst_ref=gathered.at[me * here + n, pl.ds(low, high - low), :],
                send_sem=send_1.at[j, n],
                recv_sem=recv_1.at[j, n],
                device_id={"frames": to * PLANE + spot},
            )

        def each_1(j, n, to, act):
            @pl.when(to == 0)
            def _():
                act(copy_1(j, n, REACH, plane_window))

            @pl.when(to == planes - 1)
            def _():
                act(copy_1(j, n, 0, plane_window - REACH))

            if planes > 2:

                @pl.when((to > 0) & (to < planes - 1))
                def _():
                    act(copy_1(j, n, 0, plane_window))

        def copy_2(j, n):
            first = across // PAIR * PAIR
            where = pl.ds(pl.multiple_of(first * rows, rows), pair_window)
            return pltpu.make_async_remote_copy(
                src_ref=rows_of(j, n, first, pair_window),
                dst_ref=gathered.at[frame_of(j, spot, n), where, :],
                send_sem=send_2.at[j, n],
                recv_sem=recv_2.at[j, n],
                device_id={"frames": plane * PLANE + across},
            )

        sibling_rows = pl.ds(pl.multiple_of(sibling * rows, rows), window)

        def copy_3(j, n):
            return pltpu.make_async_remote_copy(
                src_ref=rows_of(j, n, sibling, window),
                dst_ref=gathered.at[frame_of(j, spot, n), sibling_rows, :],
                send_sem=send_3.at[j, n],
                recv_sem=recv_3.at[j, n],
                device_id={"frames": plane * PLANE + sibling},
            )

        def copy_4(j, n):
            part = gathered.at[frame_of(j, across, n), sibling_rows, :]
            return pltpu.make_async_remote_copy(
                src_ref=part,
                dst_ref=part,
                send_sem=send_3.at[planes + j, n],
                recv_sem=recv_3.at[planes + j, n],
                device_id={"frames": plane * PLANE + sibling},
            )

        load_down_t.wait()
        for n in range(here):
            for part in range(chunks):
                piece(n, part).wait()
                where = slice(part * (IMG // chunks), (part + 1) * (IMG // chunks))
                half[n, where] = jnp.dot(
                    video[n, where], down_t[...], preferred_element_type=jnp.float32
                ).astype(jnp.bfloat16)
            if n == 0:
                load_down.wait()
            reduced[n, REACH : REACH + QUART, :] = jnp.dot(
                down[...], half[n], preferred_element_type=jnp.float32
            ).astype(jnp.bfloat16)
            if n == 0:
                pl.semaphore_wait(barrier, parts - 1)
            for j in range(1, planes):
                each_1(j, n, flip(plane, j), lambda copy: copy.start())
            copy_2(0, n).start()
            copy_3(0, n).start()

        lag = lax.broadcasted_iota(jnp.int32, (frames, frames), 0) - lax.broadcasted_iota(
            jnp.int32, (frames, frames), 1
        )
        toeplitz = jnp.zeros((frames, frames), jnp.float32)
        tap_row = taps[...].astype(jnp.float32)
        for k in range(min(taps.shape[1], frames)):
            toeplitz = jnp.where(lag == k, tap_row[:, k : k + 1], toeplitz)
        owner = lax.broadcasted_iota(jnp.int32, (total, frames), 0) // rows
        repeat = jnp.where(
            owner == lax.broadcasted_iota(jnp.int32, (total, frames), 1), 1.0, 0.0
        ).astype(jnp.bfloat16)
        tall = jnp.dot(
            repeat, toeplitz.astype(jnp.bfloat16), preferred_element_type=jnp.float32
        ).astype(jnp.bfloat16)
        wide = lax.dot_general(
            tall, repeat, (((1,), (1,)), ((), ())), preferred_element_type=jnp.float32
        )
        same = (
            lax.broadcasted_iota(jnp.int32, (total, total), 0) % rows
            == lax.broadcasted_iota(jnp.int32, (total, total), 1) % rows
        )
        matrix[...] = jnp.where(same, wide, 0.0).astype(jnp.bfloat16)

        def stack_one(place, block):
            stacked[place] = (
                jnp.dot(left[...], block, preferred_element_type=jnp.float32)
                .astype(jnp.bfloat16)
                .reshape(ORIENT * 2, rows, QUART)
            )

        def coefficients(where):
            for o in range(ORIENT):
                value = jnp.dot(
                    stacked[:, where, :, 2 * o].reshape(planes * here * rows, QUART),
                    right[o, 0],
                    preferred_element_type=jnp.float32,
                ) + jnp.dot(
                    stacked[:, where, :, 2 * o + 1].reshape(planes * here * rows, QUART),
                    right[o, 1],
                    preferred_element_type=jnp.float32,
                )
                value = value.astype(jnp.bfloat16).reshape(planes, here, rows, 2 * QUART)
                for p in range(planes):
                    coeffs[pl.ds((p * PLANE + where) * here, here), o] = value[p]

        own_rows = pl.ds(pl.multiple_of(spot * rows, rows), window)

        def stack_arrived(j, where):
            @pl.loop(0, here)
            def _(n):
                t = frame_of(j, where, n)
                stack_one((flip(plane, j), where, n), gathered[t, own_rows, :])

        def second(j):
            for n in range(here):
                copy_2(j, n).wait_recv()
                copy_4(j, n).start()
            stack_arrived(j, across)

        for n in range(here):
            stack_one((plane, spot, n), reduced[n, pl.ds(pl.multiple_of(me * rows, rows), window), :])
        for n in range(here):
            for j in range(1, planes):
                each_1(j, n, plane, lambda copy: copy.wait_recv())
                copy_2(j, n).start()
                copy_3(j, n).start()
        for j in range(1, planes):
            stack_arrived(j, spot)
        load_right.wait()
        for j in range(planes):
            second(j)
        coefficients(spot)
        for j in range(planes):
            for n in range(here):
                copy_3(j, n).wait_recv()
            stack_arrived(j, sibling)
        coefficients(across)
        coefficients(sibling)
        last = flip(across, 1)
        for j in range(planes):
            for n in range(here):
                copy_4(j, n).wait_recv()
            stack_arrived(j, last)
        coefficients(last)

        counts = [jnp.int32(0)] * NSEG
        for t in range(frames):
            for s in range(NSEG):
                counts[s] = counts[s] + jnp.where(segments[t] == s, 1, 0)
        picked, first = [], jnp.int32(0)
        for s in range(NSEG):
            rest = picks[s]
            for bit in reversed(range((PICK_LIMIT - 1).bit_length())):
                rest = jnp.where(rest >= counts[s] * (1 << bit), rest - counts[s] * (1 << bit), rest)
            picked.append(first + rest)
            first = first + counts[s]

        @pl.loop(0, frames)
        def _(t):
            ref = picked[NSEG - 1]
            for s in range(NSEG - 1):
                ref = jnp.where(segments[t] == s, picked[s], ref)
            ones = coeffs[t].astype(jnp.float32)
            base = coeffs[ref].astype(jnp.float32)
            real, imag = ones[..., :QUART], ones[..., QUART:]
            ref_real, ref_imag = base[..., :QUART], base[..., QUART:]
            prod_real = real * ref_real + imag * ref_imag
            prod_imag = imag * ref_real - real * ref_imag
            signal = prod_imag * lax.rsqrt(prod_real * prod_real + prod_imag * prod_imag + 1.0)
            phase[:, t] = signal.astype(jnp.bfloat16)
            denom[t] = jnp.sum(real * real + imag * imag, axis=0) + 1.0

        here_rows = pl.ds(pl.multiple_of(me * rows, rows), rows)

        def return_copy(j):
            to = peer(j)
            return pltpu.make_async_remote_copy(
                src_ref=moved.at[pl.ds(to * here, here)],
                dst_ref=out_hbm.at[:, here_rows, :],
                send_sem=send_b.at[j],
                recv_sem=recv_b.at[j],
                device_id={"frames": to},
            )

        crowd = parts // 2
        near = me // crowd

        def filter_half(number):
            span = pl.ds(number * (frames // 2), frames // 2)
            long_span = pl.ds(pl.multiple_of(number * (total // 2), total // 2), total // 2)
            for o in range(ORIENT):
                filtered = (
                    jnp.dot(
                        matrix[long_span, :],
                        phase[o].reshape(total, QUART),
                        preferred_element_type=jnp.float32,
                    )
                    .astype(jnp.bfloat16)
                    .astype(jnp.float32)
                    .reshape(frames // 2, rows, QUART)
                )
                real = coeffs[span, o, :, :QUART].astype(jnp.float32)
                imag = coeffs[span, o, :, QUART:].astype(jnp.float32)
                term = (real * real + imag * imag) * filtered
                if o == 0:
                    numer[...] = term
                elif o < ORIENT - 1:
                    numer[...] += term
                else:
                    moved[span] = ((numer[...] + term) / denom[span]).astype(jnp.bfloat16)

        filter_half(1 - near)

        @pl.loop(0, crowd)
        def _(k):
            to = (1 - near) * crowd + lax.rem(me + k, crowd)
            return_copy(lax.rem(to + parts - me, parts)).start()

        filter_half(near)

        @pl.loop(1, crowd)
        def _(k):
            to = near * crowd + lax.rem(me + k, crowd)
            return_copy(lax.rem(to + parts - me, parts)).start()

        store = pltpu.make_async_copy(
            moved.at[pl.ds(me * here, here)], out_hbm.at[:, here_rows, :], store_sem
        )
        store.start()

        for n in range(here):
            for j in range(planes):
                if j:
                    each_1(j, n, flip(plane, j), lambda copy: copy.wait_send())
                copy_2(j, n).wait_send()
                copy_3(j, n).wait_send()
                copy_4(j, n).wait_send()

        @pl.loop(1, parts)
        def _(j):
            return_copy(j).wait_recv()

        @pl.loop(1, parts)
        def _(j):
            return_copy(j).wait_send()

        store.wait()

    bf16, f32, dma = jnp.bfloat16, jnp.float32, pltpu.SemaphoreType.DMA
    anywhere = pl.BlockSpec(memory_space=pl.ANY)
    vmem = pl.BlockSpec(memory_space=pltpu.VMEM)
    smem = pl.BlockSpec(memory_space=pltpu.SMEM)
    return pl.pallas_call(
        kernel,
        out_shape=jax.ShapeDtypeStruct((here, QUART, QUART), bf16),
        in_specs=[smem, smem, vmem, anywhere, anywhere, anywhere, vmem, anywhere],
        out_specs=anywhere,
        scratch_shapes=[
            pltpu.VMEM((here, IMG, IMG), bf16),
            pltpu.VMEM((QUART, IMG), bf16),
            pltpu.VMEM((IMG, QUART), bf16),
            pltpu.VMEM((ORIENT, 2, QUART, 2 * QUART), bf16),
            pltpu.VMEM((here, IMG, QUART), bf16),
            pltpu.VMEM((here, QUART + 2 * REACH, QUART), bf16),
            pltpu.VMEM((frames, plane_window, QUART), bf16),
            pltpu.VMEM((planes, PLANE, here, ORIENT * 2, rows, QUART), bf16),
            pltpu.VMEM((frames, ORIENT, rows, 2 * QUART), bf16),
            pltpu.VMEM((ORIENT, frames, rows, QUART), bf16),
            pltpu.VMEM((total, total), bf16),
            pltpu.VMEM((frames // 2, rows, QUART), f32),
            pltpu.VMEM((frames, rows, QUART), f32),
            pltpu.VMEM((frames, rows, QUART), bf16),
            dma((3 + here * chunks,)),
            dma,
            dma((planes, here)),
            dma((planes, here)),
            dma((planes, here)),
            dma((planes, here)),
            dma((2 * planes, here)),
            dma((2 * planes, here)),
            dma((parts,)),
            dma((parts,)),
        ],
        compiler_params=pltpu.CompilerParams(
            collective_id=0, has_side_effects=True, vmem_limit_bytes=60 * 1024 * 1024
        ),
    )


def kernel_body(parts, video_frames, segments, ref_pick, band_taps):
    here = video_frames.shape[0]
    rows = QUART // parts
    down = down_table()
    return make_kernel(parts, here, rows)(
        segments,
        ref_pick,
        band_taps[None, :],
        video_frames,
        jnp.asarray(down),
        jnp.asarray(np.ascontiguousarray(down.T)),
        jnp.asarray(left_window(rows)),
        jnp.asarray(right_tables()),
    ).astype(jnp.float32)


def solution(mesh):
    parts = mesh.shape["frames"]
    if QUART % parts == 0 and (QUART // parts) % 16 == 0 and parts in (4, 8, 16):
        chosen = lambda *args: kernel_body(parts, *args)
    else:
        chosen = body
    in_specs = (P(("groups", "frames"), None, None), P("groups"), P("groups"), P())
    out_specs = P(("groups", "frames"), None, None)
    return jax.shard_map(chosen, mesh=mesh, in_specs=in_specs, out_specs=out_specs, check_vma=False)
```
